32 devices in a mesh: energy: 8 (over z, core), momentum: 4 (over y, x).
Axes of the slice: x: 2, y: 2, z: 4, core: 2. Of those that a mesh axis runs over, the one named last changes fastest.
Arguments:
- hopping: float32 [4, 2, 2, 384, 384], P('momentum'), may hold values from -0.07 to 0.07, as said below
- coupling: float32 [4, 2, 384, 384], P('momentum'), may hold values from -0.15 to 0.15
- onsite: float32 [2, 384], replicated, may hold values from -4 to -2.5
- sigma_in: float32 [8, 4, 2, 147456], P('energy', 'momentum'), may hold values from -0.12 to 0.12
- neighbor_shift: int32 [96, 48], replicated, may hold values from 1 to 95
- mode_shift: int32 [6], replicated, may hold values from 1 to 3
- phonon_kernel: float32 [6, 2, 4, 4], replicated, may hold values from -240 to 240
Outputs:
- sigma_new: float32 [8, 4, 2, 147456], P('energy', 'momentum')
The draws below stay inside these ranges and needn't reach their ends.
Inputs may be any that keep to these rules, and one draw needn't show every extreme that they name: hopping[k, c, 0] is symmetric with a zero diagonal and hopping[k, c, 1] is antisymmetric, so every cell block is Hermitian.
All inputs are finite; a program needn't handle non-finite values.
Results may differ from the reference program's by a relative error of at most 0.0003.
Values sent between devices are 32-bit elements; how exact they have to be, the bound alone decides.
A program may use at most 256 MiB of HBM per device.

```python
import jax
import jax.numpy as jnp
from jax import lax

ORB = 384
ORB_ATOM = 4
ATOMS = 96
NEIGH = 48
PAIR_COLS = 147456
MODES = 6
NS_STEPS = 2
ENERGIES = 8
MOMENTA = 4


def draw_hopping(key, part):
    first_key, second_key = jax.random.split(jax.random.fold_in(key, 11))
    array_shape = (MOMENTA, 2, ORB, ORB)
    real_draw = jax.random.uniform(first_key, array_shape, jnp.float32, -0.07, 0.07)
    imag_draw = jax.random.uniform(second_key, array_shape, jnp.float32, -0.07, 0.07)
    row_index = lax.broadcasted_iota(jnp.int32, (ORB, ORB), 0)
    col_index = lax.broadcasted_iota(jnp.int32, (ORB, ORB), 1)
    off_diagonal = (row_index != col_index).astype(jnp.float32)
    real_part = 0.5 * (real_draw + jnp.swapaxes(real_draw, -1, -2)) * off_diagonal
    imag_part = 0.5 * (imag_draw - jnp.swapaxes(imag_draw, -1, -2))
    return jnp.stack([real_part, imag_part], axis=2)


def draw_coupling(key, part):
    first_key = jax.random.fold_in(jax.random.fold_in(key, 23), 0)
    array_shape = (MOMENTA, 2, ORB, ORB)
    entries = 0.025 * jax.random.normal(first_key, array_shape, jnp.float32)
    return jnp.clip(entries, -0.15, 0.15)


def place_ends(array, key, low, high):
    shape = array.shape
    spot = [jax.random.randint(jax.random.fold_in(key, axis), (), 0, shape[axis]) for axis in range(len(shape))]
    array = array.at[tuple(spot)].set(low)
    longest = shape.index(max(shape))
    spot[longest] = (spot[longest] + 1) % shape[longest]
    return array.at[tuple(spot)].set(high)


def block_scale(rng, shape, pieces, smallest, largest):
    def one(position, parts):
        steps = jax.random.uniform(jax.random.fold_in(jax.random.fold_in(rng, 6), position), (parts,), jnp.float32, smallest / len(pieces), largest / len(pieces))
        return jnp.repeat(jnp.exp(steps), shape[position] // parts).reshape((-1,) + (1,) * (len(shape) - position - 1))

    loudness = one(*pieces[0])
    for cut in pieces[1:]:
        loudness = loudness * one(*cut)
    return loudness


def centred(key, shape, deviation, limit, cuts=(), kind=jnp.bfloat16):
    level = block_scale(key, shape, cuts, -0.22, 0.18) if cuts else 1.0
    result = jax.random.normal(key, shape, jnp.float32) * deviation * level
    return jnp.minimum(jnp.maximum(result, -limit), limit).astype(kind)


def setup_inputs(seed: int = 0) -> dict:
    key_of = jax.random.split(jax.random.key(seed), 8)
    return {
        "hopping": draw_hopping(jax.random.fold_in(key_of[7], 71), 0),
        "coupling": draw_coupling(jax.random.fold_in(key_of[7], 71), 0),
        "onsite": jnp.clip(jax.random.uniform(key_of[2], (2, ORB), jnp.float32, -4.0, -2.5), -4.0, -2.5),
        "sigma_in": centred(key_of[3], (ENERGIES, MOMENTA, 2, PAIR_COLS), 0.02, 0.12, ((0, 8), (1, 4)), jnp.float32),
        "neighbor_shift": place_ends(jax.random.randint(key_of[4], (ATOMS, NEIGH), 1, ATOMS), jax.random.fold_in(key_of[4], 1), 1, ATOMS - 1).astype(jnp.int32),
        "mode_shift": place_ends(jax.random.randint(key_of[5], (MODES,), 1, ENERGIES // 2), jax.random.fold_in(key_of[5], 1), 1, (ENERGIES // 2) - 1).astype(jnp.int32),
        "phonon_kernel": centred(key_of[6], (MODES, 2, MOMENTA, MOMENTA), 40.0, 240.0, (), jnp.float32),
    }


BROADENING = 0.5


def matmul_high(first_matrix, second_matrix):
    return jnp.dot(first_matrix, second_matrix, precision=lax.Precision.HIGHEST, preferred_element_type=jnp.float32)


def complex_product(first_pair, second_pair):
    real_real = matmul_high(first_pair[0], second_pair[0])
    imag_imag = matmul_high(first_pair[1], second_pair[1])
    summed = matmul_high(first_pair[0] + first_pair[1], second_pair[0] + second_pair[1])
    return (real_real - imag_imag, summed - real_real - imag_imag)


def newton_inverse(system):
    diagonal_real = jnp.diagonal(system[0])
    diagonal_imag = jnp.diagonal(system[1])
    magnitude = diagonal_real * diagonal_real + diagonal_imag * diagonal_imag
    inverse_real = diagonal_real / magnitude
    inverse_imag = -diagonal_imag / magnitude
    column_real = system[0] * inverse_real[None, :] - system[1] * inverse_imag[None, :]
    column_imag = system[0] * inverse_imag[None, :] + system[1] * inverse_real[None, :]
    scaled_real = inverse_real[:, None] * column_real - inverse_imag[:, None] * column_imag
    scaled_imag = inverse_real[:, None] * column_imag + inverse_imag[:, None] * column_real
    guess = (2.0 * jnp.diag(inverse_real) - scaled_real, 2.0 * jnp.diag(inverse_imag) - scaled_imag)
    for step_number in range(NS_STEPS - 1):
        product = complex_product(system, guess)
        correction = complex_product(guess, product)
        guess = (2.0 * guess[0] - correction[0], 2.0 * guess[1] - correction[1])
    return guess


def place_pairs(pair_values, row_atom, col_atom):
    entries = pair_values.reshape(ATOMS, NEIGH, 2, ORB_ATOM, ORB_ATOM)
    placed = jnp.zeros((2, ATOMS, ORB_ATOM, ATOMS, ORB_ATOM), jnp.float32).at[:, row_atom, :, col_atom, :].add(entries)
    placed = placed.reshape(2, ORB, ORB)
    return (placed[0], placed[1])


def pick_pairs(matrix_pair, row_atom, col_atom):
    stacked = jnp.stack([matrix_pair[0], matrix_pair[1]]).reshape(2, ATOMS, ORB_ATOM, ATOMS, ORB_ATOM)
    return stacked[:, row_atom, :, col_atom, :].reshape(PAIR_COLS)


def green_point(energy_real, hopping_block, coupling_block, onsite, sigma_point, row_atom, col_atom):
    identity = jnp.eye(ORB, dtype=jnp.float32)
    systems = []
    for cell_index in range(2):
        self_energy = place_pairs(sigma_point[cell_index], row_atom, col_atom)
        system_real = jnp.diag(energy_real - onsite[cell_index]) - hopping_block[cell_index, 0] - self_energy[0]
        system_imag = BROADENING * identity - hopping_block[cell_index, 1] - self_energy[1]
        systems.append((system_real, system_imag))
    first_green = newton_inverse(systems[0])
    coupling_pair = (coupling_block[0], coupling_block[1])
    coupling_adjoint = (coupling_block[0].T, -coupling_block[1].T)
    adjoint_green = complex_product(coupling_adjoint, first_green)
    folded = complex_product(adjoint_green, coupling_pair)
    second_green = newton_inverse((systems[1][0] - folded[0], systems[1][1] - folded[1]))
    green_coupling = complex_product(first_green, coupling_pair)
    through = complex_product(complex_product(green_coupling, second_green), adjoint_green)
    first_full = (first_green[0] + through[0], first_green[1] + through[1])
    return jnp.stack([pick_pairs(first_full, row_atom, col_atom), pick_pairs(second_green, row_atom, col_atom)])


def build_kernel(mode_shift, phonon_kernel, energies, momenta):
    target = lax.broadcasted_iota(jnp.int32, (MODES, energies, energies), 1)
    source = lax.broadcasted_iota(jnp.int32, (MODES, energies, energies), 2)
    shifted = mode_shift[:, None, None]
    lower = (source == target - shifted).astype(jnp.float32)
    upper = (source == target + shifted).astype(jnp.float32)
    combined = jnp.einsum("jab,jkq->akbq", lower, phonon_kernel[:, 0], precision=lax.Precision.HIGHEST)
    combined = combined + jnp.einsum("jab,jkq->akbq", upper, phonon_kernel[:, 1], precision=lax.Precision.HIGHEST)
    return combined.reshape(energies * momenta, energies * momenta)


def reference(hopping, coupling, onsite, sigma_in, neighbor_shift, mode_shift, phonon_kernel):
    row_atom = lax.broadcasted_iota(jnp.int32, (ATOMS, NEIGH), 0)
    col_atom = (row_atom + neighbor_shift) % ATOMS

    def one_point(point_index):
        energy = point_index // MOMENTA
        momentum = point_index % MOMENTA
        energy_real = 2.0 * (energy.astype(jnp.float32) + 0.5) / ENERGIES
        return green_point(energy_real, hopping[momentum], coupling[momentum], onsite, sigma_in[energy, momentum], row_atom, col_atom)

    green_pairs = lax.map(one_point, jnp.arange(ENERGIES * MOMENTA, dtype=jnp.int32))
    kernel = build_kernel(mode_shift, phonon_kernel, ENERGIES, MOMENTA)
    flattened = green_pairs.reshape(ENERGIES * MOMENTA, 2 * PAIR_COLS)
    return matmul_high(kernel, flattened).reshape(ENERGIES, MOMENTA, 2, PAIR_COLS)
```

```python
import functools

import jax
import jax.numpy as jnp
from jax import lax
from jax.experimental import pallas as pl
from jax.experimental.pallas import tpu as pltpu
from jax.sharding import PartitionSpec as P

BROADENING = 0.5
LANES = 128
F32 = jnp.float32
BF16 = jnp.bfloat16


def dot(a, b):
    return jnp.dot(a, b, preferred_element_type=F32)


def split(x):
    high = x.astype(BF16)
    return high, (x - high.astype(F32)).astype(BF16)


def point_kernel(
    dims, z_ref, pairs_ref, shift_ref, hop_ref, coup_ref, onsite_ref, out_ref,
    rows_ref, sig_ref, acc_ref, coupling, adjoint, system, guess, prod, first, second, ag,
    left_h, left_l, right_h, right_l,
):
    atoms, neigh, per_atom = dims
    orb = atoms * per_atom
    entries = 2 * per_atom * per_atom
    groups = LANES // entries
    chunks = neigh // groups
    f32_lanes = lax.broadcasted_iota(jnp.int32, (atoms, LANES), 1)

    for cell in range(2):
        for chunk in range(chunks):
            part = pairs_ref[pl.ds(2 * chunk + cell, atoms, stride=2 * chunks), :]
            rows_ref[chunk * LANES:(chunk + 1) * LANES, 0:atoms] = part.T
        for entry in range(entries):
            part = rows_ref[pl.ds(entry, neigh, stride=entries), :]
            sig_ref[cell * entries + entry, :, 0:neigh] = part.T[0:atoms]

    index = lax.broadcasted_iota(jnp.int32, (atoms, neigh), 0) + shift_ref[...].T
    index = jnp.where(index >= atoms, index - atoms, index)

    def following(previous):
        current = jnp.full((atoms, LANES), LANES, jnp.int32)
        for n in reversed(range(neigh)):
            column = jnp.broadcast_to(index[:, n:n + 1], (atoms, LANES))
            current = jnp.where((column == f32_lanes) & (n > previous), n, current)
        return current

    def gathered(block, current):
        safe = jnp.where(current < LANES, current, 0)
        value = jnp.take_along_axis(sig_ref[block], safe, axis=1)
        return jnp.where(current < LANES, value, 0.0)

    def smallest(current):
        return jnp.min(current)

    current = following(jnp.full((atoms, LANES), -1, jnp.int32))

    def store_first(block, carry):
        acc_ref[block] = gathered(block, current)
        return carry

    lax.fori_loop(0, 2 * entries, store_first, 0)

    def more(state):
        return state[1] < LANES

    def step(state):
        now = state[0]

        def add(block, carry):
            acc_ref[block] = acc_ref[block] + gathered(block, now)
            return carry

        lax.fori_loop(0, 2 * entries, add, 0)
        later = following(now)
        return later, smallest(later)

    current = following(current)
    lax.while_loop(more, step, (current, smallest(current)))

    row = lax.broadcasted_iota(jnp.int32, (orb, orb), 0)
    col = lax.broadcasted_iota(jnp.int32, (orb, orb), 1)
    eye = row == col

    def source(position):
        turn = sum((position >= atoms * k).astype(jnp.int32) for k in range(1, per_atom))
        return per_atom * (position - atoms * turn) + turn

    perm = (col == source(row)).astype(F32).astype(BF16)
    perm_t = (row == source(col)).astype(F32).astype(BF16)

    def permuted(matrix):
        high, low = split(matrix)
        moved = dot(perm, jnp.concatenate([high, low], axis=1)).astype(BF16)
        return dot(moved[:, 0:orb], perm_t) + dot(moved[:, orb:], perm_t)

    def put_left(ref):
        high, low = split(ref[...])
        left_h[...] = high
        left_l[...] = low

    def put_right(ref):
        high, low = split(ref[...])
        for part, dst in ((high, right_h), (low, right_l)):
            dst[0:orb, :] = part
            dst[orb:2 * orb, 0:orb] = -part[:, orb:]
            dst[orb:2 * orb, orb:] = part[:, 0:orb]

    width = 256 if (2 * orb) % 256 == 0 else LANES

    def product(emit):
        def tile(t, carry):
            window = pl.ds(pl.multiple_of(t * width, width), width)
            high = right_h[:, window]
            total = dot(left_h[...], right_l[:, window]) + dot(left_l[...], high)
            emit(window, total + dot(left_h[...], high))
            return carry

        lax.fori_loop(0, 2 * orb // width, tile, 0)

    def into(dst):
        def emit(window, value):
            dst[:, window] = value
        return emit

    def invert(dst):
        real, imag = system[:, 0:orb], system[:, orb:]
        own_real, own_imag = jnp.where(eye, real, 0.0), jnp.where(eye, imag, 0.0)
        pairs = []
        for axis in (0, 1):
            dr = jnp.sum(own_real, axis=axis, keepdims=True)
            di = jnp.sum(own_imag, axis=axis, keepdims=True)
            size = dr * dr + di * di
            pairs.append((dr / size, -di / size))
        (rr, ri), (cr, ci) = pairs
        col_real, col_imag = real * rr - imag * ri, real * ri + imag * rr
        guess[:, 0:orb] = jnp.where(eye, 2.0 * rr, 0.0) - (cr * col_real - ci * col_imag)
        guess[:, orb:] = jnp.where(eye, 2.0 * ri, 0.0) - (cr * col_imag + ci * col_real)
        put_left(system)
        put_right(guess)
        product(into(prod))
        put_left(guess)
        put_right(prod)

        def emit(window, value):
            dst[:, window] = 2.0 * guess[:, window] - value

        product(emit)

    def build_system(cell):
        onsite = jnp.where(eye, onsite_ref[cell:cell + 1, :], 0.0)
        system[:, 0:orb] = jnp.where(eye, z_ref[0], 0.0) - permuted(hop_ref[0, cell, 0] + onsite)
        system[:, orb:] = jnp.where(eye, BROADENING, 0.0) - permuted(hop_ref[0, cell, 1])
        for part in range(2):
            for i in range(per_atom):
                blocks = []
                for j in range(per_atom):
                    entry = ((cell * 2 + part) * per_atom + i) * per_atom + j
                    blocks.append(acc_ref[entry][:, 0:atoms])
                band = (slice(i * atoms, (i + 1) * atoms), slice(part * orb, (part + 1) * orb))
                system[band] = system[band] - jnp.concatenate(blocks, axis=1)

    coup_real, coup_imag = permuted(coup_ref[0, 0]), permuted(coup_ref[0, 1])
    coupling[:, 0:orb] = coup_real
    coupling[:, orb:] = coup_imag
    adjoint[:, 0:orb] = coup_real.T
    adjoint[:, orb:] = -coup_imag.T

    build_system(0)
    invert(first)
    put_left(adjoint)
    put_right(first)
    product(into(ag))
    build_system(1)
    put_left(ag)
    put_right(coupling)

    def fold(window, value):
        system[:, window] = system[:, window] - value

    product(fold)
    put_left(first)
    product(into(adjoint))
    invert(second)
    put_left(adjoint)
    put_right(second)
    product(into(prod))
    put_left(prod)
    put_right(ag)

    def full(window, value):
        first[:, window] = first[:, window] + value

    product(full)

    pad = jnp.zeros((atoms, LANES - neigh), jnp.int32)
    pick = jnp.concatenate([index, pad], axis=1)
    for cell, green in ((0, first), (1, second)):
        for part in range(2):
            for i in range(per_atom):
                for j in range(per_atom):
                    start = part * orb + j * atoms
                    lane = min(start, 2 * orb - LANES)
                    block = green[i * atoms:(i + 1) * atoms, lane:lane + LANES]
                    value = jnp.take_along_axis(block, pick + (start - lane), axis=1)
                    entry = (part * per_atom + i) * per_atom + j
                    value = jnp.concatenate([value, jnp.zeros((LANES - atoms, LANES), F32)], axis=0)
                    rows_ref[pl.ds(entry, neigh, stride=entries), :] = value.T[0:neigh]
        for chunk in range(chunks):
            part = rows_ref[chunk * LANES:(chunk + 1) * LANES, :].T
            out_ref[pl.ds(2 * chunk + cell, atoms, stride=2 * chunks), :] = part[0:atoms]


def green_pairs_of(energy_real, pairs, neighbor_shift, hopping, coupling, onsite, per_atom):
    neigh, atoms = neighbor_shift.shape
    orb = atoms * per_atom
    entries = 2 * per_atom * per_atom
    vmem = pl.BlockSpec(memory_space=pltpu.VMEM)
    complex_block = pltpu.VMEM((orb, 2 * orb), F32)
    return pl.pallas_call(
        functools.partial(point_kernel, (atoms, neigh, per_atom)),
        out_shape=jax.ShapeDtypeStruct(pairs.shape, F32),
        in_specs=[pl.BlockSpec(memory_space=pltpu.SMEM)] + [vmem] * 5,
        out_specs=vmem,
        scratch_shapes=[
            pltpu.VMEM((neigh * entries, LANES), F32),
            pltpu.VMEM((2 * entries, atoms, LANES), F32),
            pltpu.VMEM((2 * entries, atoms, LANES), F32),
        ]
        + [complex_block] * 8
        + [pltpu.VMEM((orb, 2 * orb), BF16)] * 2
        + [pltpu.VMEM((2 * orb, 2 * orb), BF16)] * 2,
        compiler_params=pltpu.CompilerParams(vmem_limit_bytes=60 * 1024 * 1024),
        name="point_green",
    )(energy_real, pairs, neighbor_shift, hopping, coupling, onsite)


def mix_kernel(weight_ref, x_ref, o_ref):
    points = x_ref.shape[0]

    def target(p, carry):
        total = weight_ref[p, 0] * x_ref[0]
        for q in range(1, points):
            total = total + weight_ref[p, q] * x_ref[q]
        o_ref[p] = total
        return carry

    lax.fori_loop(0, points, target, 0)


def mix(weights, received):
    return pl.pallas_call(
        mix_kernel,
        out_shape=jax.ShapeDtypeStruct(received.shape, F32),
        in_specs=[pl.BlockSpec(memory_space=pltpu.SMEM), pl.BlockSpec(memory_space=pltpu.VMEM)],
        out_specs=pl.BlockSpec(memory_space=pltpu.VMEM),
        name="mix_points",
    )(weights, received)


def build_kernel(mode_shift, phonon_kernel, energies, momenta):
    modes = mode_shift.shape[0]
    target = lax.broadcasted_iota(jnp.int32, (modes, energies, energies), 1)
    source = lax.broadcasted_iota(jnp.int32, (modes, energies, energies), 2)
    shifted = mode_shift[:, None, None]
    lower = (source == target - shifted).astype(F32)
    upper = (source == target + shifted).astype(F32)
    high = lax.Precision.HIGHEST
    combined = jnp.einsum("jab,jkq->akbq", lower, phonon_kernel[:, 0], precision=high)
    combined = combined + jnp.einsum("jab,jkq->akbq", upper, phonon_kernel[:, 1], precision=high)
    return combined.reshape(energies * momenta, energies * momenta)


def body(hopping, coupling, onsite, sigma_in, neighbor_shift, mode_shift, phonon_kernel):
    energies = sigma_in.shape[0] * lax.axis_size("energy")
    momenta = sigma_in.shape[1] * lax.axis_size("momentum")
    points = energies * momenta
    pair_cols = sigma_in.shape[3]
    atoms = neighbor_shift.shape[0]
    per_atom = onsite.shape[1] // atoms
    energy_real = 2.0 * (lax.axis_index("energy").astype(F32) + 0.5) / energies
    pairs = sigma_in.reshape(2, pair_cols // LANES, LANES).transpose(1, 0, 2)
    pairs = pairs.reshape(2 * pair_cols // LANES, LANES)
    green = green_pairs_of(
        energy_real.reshape(1), pairs, neighbor_shift.T, hopping, coupling, onsite, per_atom
    )
    weights = build_kernel(mode_shift, phonon_kernel, energies, momenta)
    blocks = green.reshape(points, 2 * pair_cols // LANES // points, LANES)
    names = ("energy", "momentum")
    received = lax.all_to_all(blocks, names, split_axis=0, concat_axis=0, tiled=True)
    mixed = mix(weights, received)
    returned = lax.all_to_all(mixed, names, split_axis=0, concat_axis=0, tiled=True)
    returned = returned.reshape(pair_cols // LANES, 2, LANES).transpose(1, 0, 2)
    return returned.reshape(1, 1, 2, pair_cols)


def solution(mesh):
    return jax.shard_map(
        body,
        mesh=mesh,
        in_specs=(
            P("momentum", None, None, None, None),
            P("momentum", None, None, None),
            P(),
            P("energy", "momentum", None, None),
            P(),
            P(),
            P(),
        ),
        out_specs=P("energy", "momentum", None, None),
        check_vma=False,
    )
```

```python
import functools

import jax
import jax.numpy as jnp
from jax import lax
from jax.experimental import pallas as pl
from jax.experimental.pallas import tpu as pltpu
from jax.sharding import PartitionSpec as P

BROADENING = 0.5
LANES = 128
F32 = jnp.float32
BF16 = jnp.bfloat16


def dot(a, b):
    return jnp.dot(a, b, preferred_element_type=F32)


def split(x):
    high = x.astype(BF16)
    return high, (x - high.astype(F32)).astype(BF16)


def point_kernel(
    dims, z_ref, pairs_ref, shift_ref, hop_ref, coup_ref, onsite_ref, out_ref,
    rows_ref, sig_ref, acc_ref, coupling, adjoint, system, guess, prod, first, second, ag,
    left_h, left_l, right_h, right_l,
):
    atoms, neigh, per_atom = dims
    orb = atoms * per_atom
    entries = 2 * per_atom * per_atom
    groups = LANES // entries
    chunks = neigh // groups
    f32_lanes = lax.broadcasted_iota(jnp.int32, (atoms, LANES), 1)

    for cell in range(2):
        for chunk in range(chunks):
            part = pairs_ref[pl.ds(2 * chunk + cell, atoms, stride=2 * chunks), :]
            rows_ref[chunk * LANES:(chunk + 1) * LANES, 0:atoms] = part.T
        for entry in range(entries):
            part = rows_ref[pl.ds(entry, neigh, stride=entries), :]
            sig_ref[cell * entries + entry, :, 0:neigh] = part.T[0:atoms]

    index = lax.broadcasted_iota(jnp.int32, (atoms, neigh), 0) + shift_ref[...].T
    index = jnp.where(index >= atoms, index - atoms, index)

    def following(previous):
        current = jnp.full((atoms, LANES), LANES, jnp.int32)
        for n in reversed(range(neigh)):
            column = jnp.broadcast_to(index[:, n:n + 1], (atoms, LANES))
            current = jnp.where((column == f32_lanes) & (n > previous), n, current)
        return current

    def gathered(block, current):
        safe = jnp.where(current < LANES, current, 0)
        value = jnp.take_along_axis(sig_ref[block], safe, axis=1)
        return jnp.where(current < LANES, value, 0.0)

    def smallest(current):
        return jnp.min(current)

    current = following(jnp.full((atoms, LANES), -1, jnp.int32))

    unroll = 8

    def store_first(group, carry):
        for u in range(unroll):
            block = group * unroll + u
            acc_ref[block] = gathered(block, current)
        return carry

    lax.fori_loop(0, 2 * entries // unroll, store_first, 0)

    def more(state):
        return state[1] < LANES

    def step(state):
        now = state[0]

        def add(group, carry):
            for u in range(unroll):
                block = group * unroll + u
                acc_ref[block] = acc_ref[block] + gathered(block, now)
            return carry

        lax.fori_loop(0, 2 * entries // unroll, add, 0)
        later = following(now)
        return later, smallest(later)

    current = following(current)
    lax.while_loop(more, step, (current, smallest(current)))

    row = lax.broadcasted_iota(jnp.int32, (orb, orb), 0)
    col = lax.broadcasted_iota(jnp.int32, (orb, orb), 1)
    eye = row == col

    def source(position):
        turn = sum((position >= atoms * k).astype(jnp.int32) for k in range(1, per_atom))
        return per_atom * (position - atoms * turn) + turn

    perm = (col == source(row)).astype(F32).astype(BF16)
    perm_t = (row == source(col)).astype(F32).astype(BF16)

    def permuted(matrix):
        high, low = split(matrix)
        moved = dot(perm, jnp.concatenate([high, low], axis=1)).astype(BF16)
        return dot(moved[:, 0:orb], perm_t) + dot(moved[:, orb:], perm_t)

    def put_left(ref):
        high, low = split(ref[...])
        left_h[...] = high
        left_l[...] = low

    def put_right(ref):
        high, low = split(ref[...])
        for part, dst in ((high, right_h), (low, right_l)):
            dst[0:orb, :] = part
            dst[orb:2 * orb, 0:orb] = -part[:, orb:]
            dst[orb:2 * orb, orb:] = part[:, 0:orb]

    width = 256 if (2 * orb) % 256 == 0 else LANES

    def product(emit):
        def tile(t, carry):
            window = pl.ds(pl.multiple_of(t * width, width), width)
            high = right_h[:, window]
            total = dot(left_h[...], right_l[:, window]) + dot(left_l[...], high)
            emit(window, total + dot(left_h[...], high))
            return carry

        lax.fori_loop(0, 2 * orb // width, tile, 0)

    def into(dst):
        def emit(window, value):
            dst[:, window] = value
        return emit

    def invert(dst):
        real, imag = system[:, 0:orb], system[:, orb:]
        own_real, own_imag = jnp.where(eye, real, 0.0), jnp.where(eye, imag, 0.0)
        pairs = []
        for axis in (0, 1):
            dr = jnp.sum(own_real, axis=axis, keepdims=True)
            di = jnp.sum(own_imag, axis=axis, keepdims=True)
            size = dr * dr + di * di
            pairs.append((dr / size, -di / size))
        (rr, ri), (cr, ci) = pairs
        col_real, col_imag = real * rr - imag * ri, real * ri + imag * rr
        guess[:, 0:orb] = jnp.where(eye, 2.0 * rr, 0.0) - (cr * col_real - ci * col_imag)
        guess[:, orb:] = jnp.where(eye, 2.0 * ri, 0.0) - (cr * col_imag + ci * col_real)
        put_left(system)
        put_right(guess)
        product(into(prod))
        put_left(guess)
        put_right(prod)

        def emit(window, value):
            dst[:, window] = 2.0 * guess[:, window] - value

        product(emit)

    def build_system(cell):
        onsite = jnp.where(eye, onsite_ref[cell:cell + 1, :], 0.0)
        system[:, 0:orb] = jnp.where(eye, z_ref[0], 0.0) - permuted(hop_ref[0, cell, 0] + onsite)
        system[:, orb:] = jnp.where(eye, BROADENING, 0.0) - permuted(hop_ref[0, cell, 1])
        for part in range(2):
            for i in range(per_atom):
                blocks = []
                for j in range(per_atom):
                    entry = ((cell * 2 + part) * per_atom + i) * per_atom + j
                    blocks.append(acc_ref[entry][:, 0:atoms])
                band = (slice(i * atoms, (i + 1) * atoms), slice(part * orb, (part + 1) * orb))
                system[band] = system[band] - jnp.concatenate(blocks, axis=1)

    coup_real, coup_imag = permuted(coup_ref[0, 0]), permuted(coup_ref[0, 1])
    coupling[:, 0:orb] = coup_real
    coupling[:, orb:] = coup_imag
    adjoint[:, 0:orb] = coup_real.T
    adjoint[:, orb:] = -coup_imag.T

    build_system(0)
    invert(first)
    put_left(adjoint)
    put_right(first)
    product(into(ag))
    build_system(1)
    put_left(ag)
    put_right(coupling)

    def fold(window, value):
        system[:, window] = system[:, window] - value

    product(fold)
    put_left(first)
    product(into(adjoint))
    invert(second)
    put_left(adjoint)
    put_right(second)
    product(into(prod))
    put_left(prod)
    put_right(ag)

    def full(window, value):
        first[:, window] = first[:, window] + value

    product(full)

    pad = jnp.zeros((atoms, LANES - neigh), jnp.int32)
    pick = jnp.concatenate([index, pad], axis=1)
    for cell, green in ((0, first), (1, second)):
        for part in range(2):
            for i in range(per_atom):
                for j in range(per_atom):
                    start = part * orb + j * atoms
                    lane = min(start, 2 * orb - LANES)
                    block = green[i * atoms:(i + 1) * atoms, lane:lane + LANES]
                    value = jnp.take_along_axis(block, pick + (start - lane), axis=1)
                    entry = (part * per_atom + i) * per_atom + j
                    value = jnp.concatenate([value, jnp.zeros((LANES - atoms, LANES), F32)], axis=0)
                    rows_ref[pl.ds(entry, neigh, stride=entries), :] = value.T[0:neigh]
        for chunk in range(chunks):
            part = rows_ref[chunk * LANES:(chunk + 1) * LANES, :].T
            out_ref[pl.ds(2 * chunk + cell, atoms, stride=2 * chunks), :] = part[0:atoms]


def green_pairs_of(energy_real, pairs, neighbor_shift, hopping, coupling, onsite, per_atom):
    neigh, atoms = neighbor_shift.shape
    orb = atoms * per_atom
    entries = 2 * per_atom * per_atom
    vmem = pl.BlockSpec(memory_space=pltpu.VMEM)
    complex_block = pltpu.VMEM((orb, 2 * orb), F32)
    return pl.pallas_call(
        functools.partial(point_kernel, (atoms, neigh, per_atom)),
        out_shape=jax.ShapeDtypeStruct(pairs.shape, F32),
        in_specs=[pl.BlockSpec(memory_space=pltpu.SMEM)] + [vmem] * 5,
        out_specs=vmem,
        scratch_shapes=[
            pltpu.VMEM((neigh * entries, LANES), F32),
            pltpu.VMEM((2 * entries, atoms, LANES), F32),
            pltpu.VMEM((2 * entries, atoms, LANES), F32),
        ]
        + [complex_block] * 8
        + [pltpu.VMEM((orb, 2 * orb), BF16)] * 2
        + [pltpu.VMEM((2 * orb, 2 * orb), BF16)] * 2,
        compiler_params=pltpu.CompilerParams(vmem_limit_bytes=60 * 1024 * 1024),
        name="point_green",
    )(energy_real, pairs, neighbor_shift, hopping, coupling, onsite)


def mix_kernel(weight_ref, x_ref, o_ref):
    points = x_ref.shape[0]

    def target(p, carry):
        total = weight_ref[p, 0] * x_ref[0]
        for q in range(1, points):
            total = total + weight_ref[p, q] * x_ref[q]
        o_ref[p] = total
        return carry

    lax.fori_loop(0, points, target, 0)


def mix(weights, received):
    return pl.pallas_call(
        mix_kernel,
        out_shape=jax.ShapeDtypeStruct(received.shape, F32),
        in_specs=[pl.BlockSpec(memory_space=pltpu.SMEM), pl.BlockSpec(memory_space=pltpu.VMEM)],
        out_specs=pl.BlockSpec(memory_space=pltpu.VMEM),
        name="mix_points",
    )(weights, received)


def build_kernel(mode_shift, phonon_kernel, energies, momenta):
    modes = mode_shift.shape[0]
    target = lax.broadcasted_iota(jnp.int32, (modes, energies, energies), 1)
    source = lax.broadcasted_iota(jnp.int32, (modes, energies, energies), 2)
    shifted = mode_shift[:, None, None]
    lower = (source == target - shifted).astype(F32)
    upper = (source == target + shifted).astype(F32)
    high = lax.Precision.HIGHEST
    combined = jnp.einsum("jab,jkq->akbq", lower, phonon_kernel[:, 0], precision=high)
    combined = combined + jnp.einsum("jab,jkq->akbq", upper, phonon_kernel[:, 1], precision=high)
    return combined.reshape(energies * momenta, energies * momenta)


def body(hopping, coupling, onsite, sigma_in, neighbor_shift, mode_shift, phonon_kernel):
    energies = sigma_in.shape[0] * lax.axis_size("energy")
    momenta = sigma_in.shape[1] * lax.axis_size("momentum")
    points = energies * momenta
    pair_cols = sigma_in.shape[3]
    atoms = neighbor_shift.shape[0]
    per_atom = onsite.shape[1] // atoms
    energy_real = 2.0 * (lax.axis_index("energy").astype(F32) + 0.5) / energies
    pairs = sigma_in.reshape(2, pair_cols // LANES, LANES).transpose(1, 0, 2)
    pairs = pairs.reshape(2 * pair_cols // LANES, LANES)
    green = green_pairs_of(
        energy_real.reshape(1), pairs, neighbor_shift.T, hopping, coupling, onsite, per_atom
    )
    weights = build_kernel(mode_shift, phonon_kernel, energies, momenta)
    blocks = green.reshape(points, 2 * pair_cols // LANES // points, LANES)
    names = ("energy", "momentum")
    received = lax.all_to_all(blocks, names, split_axis=0, concat_axis=0, tiled=True)
    mixed = mix(weights, received)
    returned = lax.all_to_all(mixed, names, split_axis=0, concat_axis=0, tiled=True)
    returned = returned.reshape(pair_cols // LANES, 2, LANES).transpose(1, 0, 2)
    return returned.reshape(1, 1, 2, pair_cols)


def solution(mesh):
    return jax.shard_map(
        body,
        mesh=mesh,
        in_specs=(
            P("momentum", None, None, None, None),
            P("momentum", None, None, None),
            P(),
            P("energy", "momentum", None, None),
            P(),
            P(),
            P(),
        ),
        out_specs=P("energy", "momentum", None, None),
        check_vma=False,
    )
```

```python
import functools

import jax
import jax.numpy as jnp
from jax import lax
from jax.experimental import pallas as pl
from jax.experimental.pallas import tpu as pltpu
from jax.sharding import PartitionSpec as P

BROADENING = 0.5
LANES = 128
F32 = jnp.float32
BF16 = jnp.bfloat16


def dot(a, b):
    return jnp.dot(a, b, preferred_element_type=F32)


def split(x):
    high = x.astype(BF16)
    return high, (x - high.astype(F32)).astype(BF16)


def point_kernel(
    dims, z_ref, pairs_ref, shift_ref, hop_ref, coup_ref, onsite_ref, out_ref,
    rows_ref, sig_ref, acc_ref, coupling, adjoint, system, guess, prod, first, second, ag,
    left_h, left_l, right_h, right_l,
):
    atoms, neigh, per_atom = dims
    orb = atoms * per_atom
    entries = 2 * per_atom * per_atom
    groups = LANES // entries
    chunks = neigh // groups
    f32_lanes = lax.broadcasted_iota(jnp.int32, (atoms, LANES), 1)

    for cell in range(2):
        for chunk in range(chunks):
            part = pairs_ref[pl.ds(2 * chunk + cell, atoms, stride=2 * chunks), :]
            rows_ref[chunk * LANES:(chunk + 1) * LANES, 0:atoms] = part.T
        for entry in range(entries):
            part = rows_ref[pl.ds(entry, neigh, stride=entries), :]
            sig_ref[cell * entries + entry, :, 0:neigh] = part.T[0:atoms]

    index = lax.broadcasted_iota(jnp.int32, (atoms, neigh), 0) + shift_ref[...].T
    index = jnp.where(index >= atoms, index - atoms, index)

    def following(previous):
        current = jnp.full((atoms, LANES), LANES, jnp.int32)
        for n in reversed(range(neigh)):
            column = jnp.broadcast_to(index[:, n:n + 1], (atoms, LANES))
            current = jnp.where((column == f32_lanes) & (n > previous), n, current)
        return current

    def gathered(block, current):
        safe = jnp.where(current < LANES, current, 0)
        value = jnp.take_along_axis(sig_ref[block], safe, axis=1)
        return jnp.where(current < LANES, value, 0.0)

    def smallest(current):
        return jnp.min(current)

    current = following(jnp.full((atoms, LANES), -1, jnp.int32))

    unroll = 8

    def store_first(group, carry):
        for u in range(unroll):
            block = group * unroll + u
            acc_ref[block] = gathered(block, current)
        return carry

    lax.fori_loop(0, 2 * entries // unroll, store_first, 0)

    def more(state):
        return state[1] < LANES

    def step(state):
        now = state[0]

        def add(group, carry):
            for u in range(unroll):
                block = group * unroll + u
                acc_ref[block] = acc_ref[block] + gathered(block, now)
            return carry

        lax.fori_loop(0, 2 * entries // unroll, add, 0)
        later = following(now)
        return later, smallest(later)

    current = following(current)
    lax.while_loop(more, step, (current, smallest(current)))

    row = lax.broadcasted_iota(jnp.int32, (orb, orb), 0)
    col = lax.broadcasted_iota(jnp.int32, (orb, orb), 1)
    eye = row == col

    def source(position):
        turn = sum((position >= atoms * k).astype(jnp.int32) for k in range(1, per_atom))
        return per_atom * (position - atoms * turn) + turn

    perm = (col == source(row)).astype(F32).astype(BF16)
    perm_t = (row == source(col)).astype(F32).astype(BF16)

    def permuted(matrix):
        high, low = split(matrix)
        moved = dot(perm, jnp.concatenate([high, low], axis=1)).astype(BF16)
        return dot(moved[:, 0:orb], perm_t) + dot(moved[:, orb:], perm_t)

    def put_left(ref):
        high, low = split(ref[...])
        left_h[...] = high
        left_l[...] = low

    def put_right(ref):
        high, low = split(ref[...])
        for part, dst in ((high, right_h), (low, right_l)):
            dst[0:orb, :] = part
            dst[orb:2 * orb, 0:orb] = -part[:, orb:]
            dst[orb:2 * orb, orb:] = part[:, 0:orb]

    width = 256 if (2 * orb) % 256 == 0 else LANES

    def product(emit):
        for t in range(2 * orb // width):
            window = slice(t * width, (t + 1) * width)
            high = right_h[:, window]
            total = dot(left_h[...], right_l[:, window]) + dot(left_l[...], high)
            emit(window, total + dot(left_h[...], high))

    def into(dst):
        def emit(window, value):
            dst[:, window] = value
        return emit

    def invert(dst):
        real, imag = system[:, 0:orb], system[:, orb:]
        own_real, own_imag = jnp.where(eye, real, 0.0), jnp.where(eye, imag, 0.0)
        pairs = []
        for axis in (0, 1):
            dr = jnp.sum(own_real, axis=axis, keepdims=True)
            di = jnp.sum(own_imag, axis=axis, keepdims=True)
            size = dr * dr + di * di
            pairs.append((dr / size, -di / size))
        (rr, ri), (cr, ci) = pairs
        col_real, col_imag = real * rr - imag * ri, real * ri + imag * rr
        guess[:, 0:orb] = jnp.where(eye, 2.0 * rr, 0.0) - (cr * col_real - ci * col_imag)
        guess[:, orb:] = jnp.where(eye, 2.0 * ri, 0.0) - (cr * col_imag + ci * col_real)
        put_left(system)
        put_right(guess)
        product(into(prod))
        put_left(guess)
        put_right(prod)

        def emit(window, value):
            dst[:, window] = 2.0 * guess[:, window] - value

        product(emit)

    def build_system(cell):
        onsite = jnp.where(eye, onsite_ref[cell:cell + 1, :], 0.0)
        system[:, 0:orb] = jnp.where(eye, z_ref[0], 0.0) - permuted(hop_ref[0, cell, 0] + onsite)
        system[:, orb:] = jnp.where(eye, BROADENING, 0.0) - permuted(hop_ref[0, cell, 1])
        for part in range(2):
            for i in range(per_atom):
                blocks = []
                for j in range(per_atom):
                    entry = ((cell * 2 + part) * per_atom + i) * per_atom + j
                    blocks.append(acc_ref[entry][:, 0:atoms])
                band = (slice(i * atoms, (i + 1) * atoms), slice(part * orb, (part + 1) * orb))
                system[band] = system[band] - jnp.concatenate(blocks, axis=1)

    coup_real, coup_imag = permuted(coup_ref[0, 0]), permuted(coup_ref[0, 1])
    coupling[:, 0:orb] = coup_real
    coupling[:, orb:] = coup_imag
    adjoint[:, 0:orb] = coup_real.T
    adjoint[:, orb:] = -coup_imag.T

    build_system(0)
    invert(first)
    put_left(adjoint)
    put_right(first)
    product(into(ag))
    build_system(1)
    put_left(ag)
    put_right(coupling)

    def fold(window, value):
        system[:, window] = system[:, window] - value

    product(fold)
    put_left(first)
    product(into(adjoint))
    invert(second)
    put_left(adjoint)
    put_right(second)
    product(into(prod))
    put_left(prod)
    put_right(ag)

    def full(window, value):
        first[:, window] = first[:, window] + value

    product(full)

    pad = jnp.zeros((atoms, LANES - neigh), jnp.int32)
    pick = jnp.concatenate([index, pad], axis=1)
    for cell, green in ((0, first), (1, second)):
        for part in range(2):
            for i in range(per_atom):
                for j in range(per_atom):
                    start = part * orb + j * atoms
                    lane = min(start, 2 * orb - LANES)
                    block = green[i * atoms:(i + 1) * atoms, lane:lane + LANES]
                    value = jnp.take_along_axis(block, pick + (start - lane), axis=1)
                    entry = (part * per_atom + i) * per_atom + j
                    value = jnp.concatenate([value, jnp.zeros((LANES - atoms, LANES), F32)], axis=0)
                    rows_ref[pl.ds(entry, neigh, stride=entries), :] = value.T[0:neigh]
        for chunk in range(chunks):
            part = rows_ref[chunk * LANES:(chunk + 1) * LANES, :].T
            out_ref[pl.ds(2 * chunk + cell, atoms, stride=2 * chunks), :] = part[0:atoms]


def green_pairs_of(energy_real, pairs, neighbor_shift, hopping, coupling, onsite, per_atom):
    neigh, atoms = neighbor_shift.shape
    orb = atoms * per_atom
    entries = 2 * per_atom * per_atom
    vmem = pl.BlockSpec(memory_space=pltpu.VMEM)
    complex_block = pltpu.VMEM((orb, 2 * orb), F32)
    return pl.pallas_call(
        functools.partial(point_kernel, (atoms, neigh, per_atom)),
        out_shape=jax.ShapeDtypeStruct(pairs.shape, F32),
        in_specs=[pl.BlockSpec(memory_space=pltpu.SMEM)] + [vmem] * 5,
        out_specs=vmem,
        scratch_shapes=[
            pltpu.VMEM((neigh * entries, LANES), F32),
            pltpu.VMEM((2 * entries, atoms, LANES), F32),
            pltpu.VMEM((2 * entries, atoms, LANES), F32),
        ]
        + [complex_block] * 8
        + [pltpu.VMEM((orb, 2 * orb), BF16)] * 2
        + [pltpu.VMEM((2 * orb, 2 * orb), BF16)] * 2,
        compiler_params=pltpu.CompilerParams(vmem_limit_bytes=60 * 1024 * 1024),
        name="point_green",
    )(energy_real, pairs, neighbor_shift, hopping, coupling, onsite)


def mix_kernel(weight_ref, x_ref, o_ref):
    points = x_ref.shape[0]

    def target(p, carry):
        total = weight_ref[p, 0] * x_ref[0]
        for q in range(1, points):
            total = total + weight_ref[p, q] * x_ref[q]
        o_ref[p] = total
        return carry

    lax.fori_loop(0, points, target, 0)


def mix(weights, received):
    return pl.pallas_call(
        mix_kernel,
        out_shape=jax.ShapeDtypeStruct(received.shape, F32),
        in_specs=[pl.BlockSpec(memory_space=pltpu.SMEM), pl.BlockSpec(memory_space=pltpu.VMEM)],
        out_specs=pl.BlockSpec(memory_space=pltpu.VMEM),
        name="mix_points",
    )(weights, received)


def build_kernel(mode_shift, phonon_kernel, energies, momenta):
    modes = mode_shift.shape[0]
    target = lax.broadcasted_iota(jnp.int32, (modes, energies, energies), 1)
    source = lax.broadcasted_iota(jnp.int32, (modes, energies, energies), 2)
    shifted = mode_shift[:, None, None]
    lower = (source == target - shifted).astype(F32)
    upper = (source == target + shifted).astype(F32)
    high = lax.Precision.HIGHEST
    combined = jnp.einsum("jab,jkq->akbq", lower, phonon_kernel[:, 0], precision=high)
    combined = combined + jnp.einsum("jab,jkq->akbq", upper, phonon_kernel[:, 1], precision=high)
    return combined.reshape(energies * momenta, energies * momenta)


def body(hopping, coupling, onsite, sigma_in, neighbor_shift, mode_shift, phonon_kernel):
    energies = sigma_in.shape[0] * lax.axis_size("energy")
    momenta = sigma_in.shape[1] * lax.axis_size("momentum")
    points = energies * momenta
    pair_cols = sigma_in.shape[3]
    atoms = neighbor_shift.shape[0]
    per_atom = onsite.shape[1] // atoms
    energy_real = 2.0 * (lax.axis_index("energy").astype(F32) + 0.5) / energies
    pairs = sigma_in.reshape(2, pair_cols // LANES, LANES).transpose(1, 0, 2)
    pairs = pairs.reshape(2 * pair_cols // LANES, LANES)
    green = green_pairs_of(
        energy_real.reshape(1), pairs, neighbor_shift.T, hopping, coupling, onsite, per_atom
    )
    weights = build_kernel(mode_shift, phonon_kernel, energies, momenta)
    blocks = green.reshape(points, 2 * pair_cols // LANES // points, LANES)
    names = ("energy", "momentum")
    received = lax.all_to_all(blocks, names, split_axis=0, concat_axis=0, tiled=True)
    mixed = mix(weights, received)
    returned = lax.all_to_all(mixed, names, split_axis=0, concat_axis=0, tiled=True)
    returned = returned.reshape(pair_cols // LANES, 2, LANES).transpose(1, 0, 2)
    return returned.reshape(1, 1, 2, pair_cols)


def solution(mesh):
    return jax.shard_map(
        body,
        mesh=mesh,
        in_specs=(
            P("momentum", None, None, None, None),
            P("momentum", None, None, None),
            P(),
            P("energy", "momentum", None, None),
            P(),
            P(),
            P(),
        ),
        out_specs=P("energy", "momentum", None, None),
        check_vma=False,
    )
```
